128 devices in a mesh: row: 16 (over x, y), col: 8 (over z, core).
Axes of the slice: x: 4, y: 4, z: 4, core: 2. Of those that a mesh axis runs over, the one named last changes fastest.
Arguments:
- features: bfloat16 [49152, 256], P(('row', 'col')), may hold values from -6 to 6
- weight: bfloat16 [256, 256], replicated, may hold values from -0.375 to 0.375
- out_bias: float32 [256], replicated, may hold values from -3 to 3
- cotangent: bfloat16 [49152, 256], P(('row', 'col')), may hold values from -6 to 6
- adj_tiles: bfloat16 [16, 8, 24, 16, 128, 128], P('row', 'col'), may hold values from -0.125 to 0.125
- tile_cols: int32 [16, 8, 24, 16], P('row', 'col'), may hold values from 0 to 47, as said below
- tile_counts: int32 [16, 8, 24], P('row', 'col'), may hold values from 1 to 16, as said below
Outputs:
- activated: bfloat16 [49152, 256], P(('row', 'col'))
- grad_features: bfloat16 [49152, 256], P(('row', 'col'))
- grad_weight: float32 [256, 256], replicated
- grad_bias: float32 [256], replicated
The draws below stay inside these ranges and needn't reach their ends.
Inputs may be any that keep to these rules, and one draw needn't show every extreme that they name: `tile_cols`: within a tile row of a block the 16 column numbers are distinct. `tile_counts`: every block has a tile row whose 16 slots are all live.
All inputs are finite; a program needn't handle non-finite values.
Results may differ from the reference program's by a relative error of at most 0.02.
Values may be sent and summed in bfloat16 or wider, within the bound.
No kernel may reach another device: no remote copies, remote signals or barrier semaphores. Data moves between devices by JAX's collectives and lax.ppermute only.
A program may use at most 192 MiB of HBM per device.

```python
import jax
import jax.numpy as jnp
from jax import lax

F = 256
TILE = 128
K = 16
ND = 384
ROW_BLOCKS = 16
COL_BLOCKS = 8
NODES = 49152
TR = 24
TC = 48


def draw_tile_cols(key, part):
    shape_all = (ROW_BLOCKS, COL_BLOCKS, TR, TC)
    scores = jax.random.randint(key, shape_all, 0, 1 << 20) * TC + lax.broadcasted_iota(jnp.int32, shape_all, 3)
    ordering = jnp.argsort(scores, axis=3)
    return ordering[..., :K].astype(jnp.int32)


def draw_tile_counts(key, part):
    first_key, second_key, third_key = jax.random.split(key, 3)
    lowest = max(1, K // 4)
    highest = jax.random.randint(first_key, (ROW_BLOCKS, COL_BLOCKS, 1), lowest, K + 1)
    bottom = jnp.maximum(highest // 2, 1)
    raw_draw = jax.random.randint(second_key, (ROW_BLOCKS, COL_BLOCKS, TR), 0, 1 << 20)
    counted = bottom + raw_draw % (highest - bottom + 1)
    full_row = jax.random.randint(third_key, (ROW_BLOCKS, COL_BLOCKS, 1), 0, TR)
    row_iota = lax.broadcasted_iota(jnp.int32, (ROW_BLOCKS, COL_BLOCKS, TR), 2)
    return jnp.where(row_iota == full_row, K, counted).astype(jnp.int32)


def block_scale(stream_key, shape, shards, least, top_value):
    factor_of = 1.0
    for position, shards_of in shards:
        steps = jax.random.uniform(jax.random.fold_in(jax.random.fold_in(stream_key, 6), position), (shards_of,), jnp.float32, least / len(shards), top_value / len(shards))
        factor_of = factor_of * jnp.repeat(jnp.exp(steps), shape[position] // shards_of).reshape((-1,) + (1,) * (len(shape) - 1 - position))
    return factor_of


def centred(key, dims, deviation, limit, pieces=(), kind=jnp.bfloat16):
    loudness = block_scale(key, dims, pieces, -0.22, 0.18) if pieces else 1.0
    drawn = jax.random.normal(key, dims, jnp.float32) * deviation * loudness
    return jnp.minimum(jnp.maximum(drawn, -limit), limit).astype(kind)


def setup_inputs(seed: int = 0) -> dict:
    key_of = jax.random.split(jax.random.key(seed), 8)
    return {
        "features": centred(key_of[0], (NODES, F), 1.0, 6.0, ((0, 128),)),
        "weight": centred(key_of[1], (F, F), F ** -0.5, 0.375),
        "out_bias": centred(key_of[2], (F,), 0.5, 3.0, (), jnp.float32),
        "cotangent": centred(key_of[3], (NODES, F), 1.0, 6.0, ((0, 128),)),
        "adj_tiles": centred(key_of[4], (ROW_BLOCKS, COL_BLOCKS, TR, K, TILE, TILE), (K * TILE) ** -0.5, 0.125, ((0, 16), (1, 8))),
        "tile_cols": draw_tile_cols(jax.random.fold_in(key_of[7], 71), 0),
        "tile_counts": draw_tile_counts(jax.random.fold_in(key_of[7], 71), 0),
    }


def reference(features, weight, out_bias, cotangent, adj_tiles, tile_cols, tile_counts):
    feat_width = features.shape[1]
    nodes_all = features.shape[0]
    block_count = ROW_BLOCKS * COL_BLOCKS
    projected = jnp.dot(features, weight, preferred_element_type=jnp.float32).astype(jnp.bfloat16)
    proj_four = projected.reshape(ROW_BLOCKS, COL_BLOCKS, ND, feat_width)
    panels = jnp.transpose(proj_four, (1, 0, 2, 3)).reshape(COL_BLOCKS, TC, TILE, feat_width)
    slot_iota = lax.broadcasted_iota(jnp.int32, (ROW_BLOCKS, COL_BLOCKS, TR, K), 3)
    live_mask = (slot_iota < tile_counts[..., None]).astype(jnp.float32).reshape(block_count, TR, K)
    flat_tiles = adj_tiles.reshape(block_count, TR, K, TILE, TILE)
    flat_cols = tile_cols.reshape(block_count, TR, K)
    block_ids = jnp.arange(block_count, dtype=jnp.int32)

    def forward_block(inputs):
        block_vals, cols_block, live_block, ident = inputs
        col_index = (ident % COL_BLOCKS).astype(jnp.int32)
        gathered = lax.dynamic_index_in_dim(panels, col_index, 0, keepdims=False)
        picked = gathered[cols_block].astype(jnp.float32)
        masked = block_vals.astype(jnp.float32) * live_block[:, :, None, None]
        return jnp.einsum('tkab,tkbf->taf', masked, picked).astype(jnp.bfloat16)

    partial_value = lax.map(forward_block, (flat_tiles, flat_cols, live_mask, block_ids))
    partial_value = lax.optimization_barrier(partial_value).astype(jnp.float32)
    summed = partial_value.reshape(ROW_BLOCKS, COL_BLOCKS, TR * TILE, feat_width).sum(axis=1)
    preact = summed.reshape(nodes_all, feat_width) + out_bias
    sigmoid_val = jax.nn.sigmoid(preact)
    activated = (preact * sigmoid_val).astype(jnp.bfloat16)
    grad_preact = (cotangent.astype(jnp.float32) * sigmoid_val * (1.0 + preact * (1.0 - sigmoid_val))).astype(jnp.bfloat16)
    grad_rows = grad_preact.reshape(ROW_BLOCKS, TR, TILE, feat_width)

    def backward_block(inputs):
        block_vals, cols_block, live_block, ident = inputs
        row_index = (ident // COL_BLOCKS).astype(jnp.int32)
        rows_here = lax.dynamic_index_in_dim(grad_rows, row_index, 0, keepdims=False).astype(jnp.float32)
        masked = block_vals.astype(jnp.float32) * live_block[:, :, None, None]
        products = jnp.einsum('tkab,taf->tkbf', masked, rows_here)
        running = jnp.zeros((TC, TILE, feat_width), jnp.float32).at[cols_block].add(products)
        return running.astype(jnp.bfloat16)

    back = lax.map(backward_block, (flat_tiles, flat_cols, live_mask, block_ids))
    back = lax.optimization_barrier(back).astype(jnp.float32)
    column_total = back.reshape(ROW_BLOCKS, COL_BLOCKS, TC * TILE, feat_width).sum(axis=0)
    column_total = column_total.reshape(COL_BLOCKS, ROW_BLOCKS, ND, feat_width)
    grad_projected = jnp.transpose(column_total, (1, 0, 2, 3)).reshape(nodes_all, feat_width).astype(jnp.bfloat16)
    grad_features = jnp.dot(grad_projected, weight.T, preferred_element_type=jnp.float32).astype(jnp.bfloat16)
    scale_factor = nodes_all ** -0.5
    grad_weight = jnp.dot(features.T, grad_projected, preferred_element_type=jnp.float32) * scale_factor
    grad_bias = jnp.sum(grad_preact.astype(jnp.float32), axis=0) * scale_factor
    return (activated, grad_features, grad_weight, grad_bias)
```

```python
import functools

import jax
import jax.numpy as jnp
from jax import lax
from jax.experimental import pallas as pl
from jax.experimental.pallas import tpu as pltpu
from jax.sharding import PartitionSpec as P


TILE = 128
SLOTS = 16
SIDE = 4
ND = 384
HALF = 192
PER = ND // TILE
DUMMY = SIDE * SIDE * PER
WROWS = 64
WHALF = 32
BROWS = 16
BF = jnp.bfloat16
F32 = jnp.float32
VM = pl.BlockSpec(memory_space=pltpu.VMEM)


def send_row(value, dx, dy):
    pairs = []
    for x in range(SIDE):
        for y in range(SIDE):
            pairs.append((x * SIDE + y, (x + dx) % SIDE * SIDE + (y + dy) % SIDE))
    return lax.ppermute(value, "row", pairs)


def send_col(value, dz, dk):
    pairs = []
    for z in range(SIDE):
        for k in range(2):
            pairs.append((z * 2 + k, (z + dz) % SIDE * 2 + (k ^ dk)))
    return lax.ppermute(value, "col", pairs)


def rel(i, j):
    return (i % SIDE) * SIDE + j % SIDE


def params(mb=56):
    return pltpu.CompilerParams(vmem_limit_bytes=mb * 1024 * 1024)


def sum4(a, b, c, d):
    return (a + c) + (b + d)


def pack_bias(total):
    hi = total.astype(BF)
    lo = (total - hi.astype(F32)).astype(BF)
    rows = lax.broadcasted_iota(jnp.int32, (BROWS, total.shape[1]), 0)
    zero = jnp.zeros((BROWS, total.shape[1]), F32)
    return jnp.where(rows == 0, hi.astype(F32), jnp.where(rows == 1, lo.astype(F32), zero)).astype(BF)


def unpack_bias(rows):
    return jnp.sum(rows.astype(F32), axis=0, keepdims=True)


def forward_kernel(order, index, adj, own, x1, x2, x3, y1, y2, y3, yb1, yb2, yb3, xb1, xb2, xb3, swap, keep, panel):
    step = pl.program_id(0)

    @pl.when(step == 0)
    def _():
        panel[0:ND, :] = own[...]
        for i, ref in ((1, x1), (2, x2), (3, x3)):
            panel[rel(i, 0) * ND:rel(i, 0) * ND + ND, :] = ref[...]
        for j, ref in ((1, y1), (2, y2), (3, y3)):
            panel[rel(0, j) * ND:rel(0, j) * ND + ND, :] = ref[...]
        for j, ref in ((1, yb1), (2, yb2), (3, yb3)):
            for i in (1, 2, 3):
                base = rel(i, j) * ND
                panel[base:base + HALF, :] = ref[(i - 1) * HALF:i * HALF, :]
        for i, ref in ((1, xb1), (2, xb2), (3, xb3)):
            for j in (1, 2, 3):
                base = rel(i, j) * ND + HALF
                panel[base:base + HALF, :] = ref[(j - 1) * HALF:j * HALF, :]
        panel[DUMMY * TILE:, :] = jnp.zeros((TILE, panel.shape[1]), BF)

    def rows(i):
        base = (order[step] * PER + i) * SLOTS
        total = None
        for pair in range(SLOTS // 2):
            picked = []
            for half in range(2):
                start = pl.multiple_of(index[base + 2 * pair + half] * TILE, TILE)
                picked.append(panel[pl.ds(start, TILE), :])
            left = jnp.concatenate([adj[i, 2 * pair], adj[i, 2 * pair + 1]], axis=1)
            right = jnp.concatenate(picked, axis=0)
            product = jnp.dot(left, right, preferred_element_type=F32)
            total = product if total is None else total + product
        return total.astype(BF)

    results = [rows(i) for i in range(PER)]

    @pl.when(step < SIDE)
    def _():
        for i in range(PER):
            swap[0, i * TILE:(i + 1) * TILE, :] = results[i]

    @pl.when(step >= SIDE)
    def _():
        for i in range(PER):
            keep[0, i * TILE:(i + 1) * TILE, :] = results[i]


def forward(order, index, adj, pieces):
    width = pieces[0].shape[1]
    shape = jax.ShapeDtypeStruct((SIDE, ND, width), BF)
    return pl.pallas_call(
        forward_kernel,
        out_shape=(shape, shape),
        grid_spec=pltpu.PrefetchScalarGridSpec(
            num_scalar_prefetch=2,
            grid=(2 * SIDE,),
            in_specs=[pl.BlockSpec((PER, SLOTS, TILE, TILE), lambda s, o, n: (o[s], 0, 0, 0))] + [VM] * len(pieces),
            out_specs=[
                pl.BlockSpec((1, ND, width), lambda s, o, n: (jnp.minimum(s, SIDE - 1), 0, 0)),
                pl.BlockSpec((1, ND, width), lambda s, o, n: (jnp.maximum(s - SIDE, 0), 0, 0)),
            ],
            scratch_shapes=[pltpu.VMEM(((DUMMY + 1) * TILE, width), BF)],
        ),
        compiler_params=params(),
        name="forward",
    )(order, index, adj, *pieces)


def activation_kernel(zpos, keep, recv, r1, r2, r3, weight, bias, cot, act, m0, m1, m2, m3, wpart):
    agg = keep[0].astype(F32) + recv[0].astype(F32)
    for ref in (r1, r2, r3):
        agg = agg + ref[...].astype(F32)
    agg16 = agg.astype(BF)
    pre = jnp.dot(agg16, weight[...], preferred_element_type=F32) + bias[...]
    sig = 1.0 / (1.0 + jnp.exp(-pre))
    act[...] = (pre * sig).astype(BF)
    grad = (cot[...].astype(F32) * sig * (1.0 + pre * (1.0 - sig))).astype(BF)
    wpart[...] = lax.dot_general(agg16, grad, (((0,), (0,)), ((), ())), preferred_element_type=F32)
    packed = pack_bias(jnp.sum(grad.astype(F32), axis=0, keepdims=True))
    for dz, ref in enumerate((m0, m1, m2, m3)):
        ref[0:ND, :] = grad
        start = pl.multiple_of(lax.rem(zpos[0] + dz, SIDE) * WROWS, WROWS)
        ref[ND:ND + WROWS, :] = wpart[pl.ds(start, WROWS), :].astype(BF)
        ref[ND + WROWS:, :] = packed


def activation(zpos, keep, recv, parts, weight, bias, cot):
    width = cot.shape[1]
    message = jax.ShapeDtypeStruct((ND + WROWS + BROWS, width), BF)
    return pl.pallas_call(
        activation_kernel,
        out_shape=(jax.ShapeDtypeStruct(cot.shape, BF),) + (message,) * 4,
        in_specs=[pl.BlockSpec(memory_space=pltpu.SMEM)] + [VM] * 8,
        out_specs=(VM,) * 5,
        scratch_shapes=[pltpu.VMEM((width, width), F32)],
        compiler_params=params(),
        name="activation",
    )(zpos, keep, recv, *parts, weight, bias, cot)


def backward_kernel(order, index, adj, *refs):
    sources, (ym, xm, ox, oy, o00), (turned, acc) = refs[:8], (refs[8:11], refs[11:14], refs[14:17], refs[17:20], refs[20]), refs[21:]
    step = pl.program_id(0)

    @pl.when(step == 0)
    def _():
        for s, ref in enumerate(sources):
            for i in range(PER):
                turned[s * PER + i] = ref[i * TILE:(i + 1) * TILE, :].T
        acc[...] = jnp.zeros_like(acc)

    for i in range(PER):
        base = (order[step] * PER + i) * SLOTS
        left = turned[step * PER + i]
        for pair in range(SLOTS // 2):
            right = jnp.concatenate([adj[i, 2 * pair], adj[i, 2 * pair + 1]], axis=1)
            product = jnp.dot(left, right, preferred_element_type=F32)
            first = index[base + 2 * pair]
            second = index[base + 2 * pair + 1]
            acc[first] = acc[first] + product[:, :TILE]
            acc[second] = acc[second] + product[:, TILE:]

    @pl.when(step == 2 * SIDE - 1)
    def _():
        def tile(i, j, n):
            return acc[rel(-i, -j) * PER + n].T.astype(BF)

        def block(ref, i, j):
            for n in range(PER):
                ref[n * TILE:(n + 1) * TILE, :] = tile(i, j, n)

        mid = TILE // 2
        for i in (1, 2, 3):
            for j in (1, 2, 3):
                middle = tile(i, j, 1)
                base = (i - 1) * HALF
                ym[j - 1][base:base + TILE, :] = tile(i, j, 0)
                ym[j - 1][base + TILE:base + HALF, :] = middle[:mid, :]
                base = (j - 1) * HALF
                xm[i - 1][base:base + mid, :] = middle[mid:, :]
                xm[i - 1][base + mid:base + HALF, :] = tile(i, j, 2)
        for i in (1, 2, 3):
            block(ox[i - 1], i, 0)
            block(oy[i - 1], 0, i)
        block(o00, 0, 0)
        pieces = []
        for dz in range(SIDE):
            pieces.append(sources[dz][ND:, :].astype(F32) + sources[SIDE + dz][ND:, :].astype(F32))
        total = sum4(*pieces)
        packed = pack_bias(jnp.sum(total[WROWS:], axis=0, keepdims=True))
        for n in range(3):
            ym[n][3 * HALF:3 * HALF + WHALF, :] = total[:WHALF].astype(BF)
            ym[n][3 * HALF + WHALF:, :] = packed
            xm[n][3 * HALF:, :] = total[WHALF:WROWS].astype(BF)


def backward(order, index, adj, sources):
    width = sources[0].shape[1]
    ym = jax.ShapeDtypeStruct((3 * HALF + WHALF + BROWS, width), BF)
    xm = jax.ShapeDtypeStruct((3 * HALF + WHALF, width), BF)
    block = jax.ShapeDtypeStruct((ND, width), BF)
    outs = pl.pallas_call(
        backward_kernel,
        out_shape=(ym,) * 3 + (xm,) * 3 + (block,) * 7,
        grid_spec=pltpu.PrefetchScalarGridSpec(
            num_scalar_prefetch=2,
            grid=(2 * SIDE,),
            in_specs=[pl.BlockSpec((PER, SLOTS, TILE, TILE), lambda s, o, n: (o[s], 0, 0, 0))] + [VM] * 8,
            out_specs=[VM] * 13,
            scratch_shapes=[
                pltpu.VMEM((2 * SIDE * PER, width, TILE), BF),
                pltpu.VMEM((DUMMY + 1, width, TILE), F32),
            ],
        ),
        compiler_params=params(),
        name="backward",
    )(order, index, adj, *sources)
    return outs[0:3], outs[3:6], outs[6:9], outs[9:12], outs[12]


def relay_kernel(first, has_bias, own_message, r1, r2, r3, b1, b2, b3, o1, o2, o3):
    here = 0 if first else HALF
    there = HALF - here
    for n, (block, out) in enumerate(((b1, o1), (b2, o2), (b3, o3))):
        total = block[here:here + HALF, :].astype(F32)
        for ref in (r1, r2, r3):
            total = total + ref[n * HALF:(n + 1) * HALF, :].astype(F32)
        out[here:here + HALF, :] = total.astype(BF)
        out[there:there + HALF, :] = block[there:there + HALF, :]
    terms = sum4(*(ref[3 * HALF:, :].astype(F32) for ref in (own_message, r1, r2, r3)))
    weight_part = terms[:WHALF].astype(BF)
    for out in (o1, o2, o3):
        out[ND:ND + WHALF, :] = weight_part
    if has_bias:
        packed = pack_bias(jnp.sum(terms[WHALF:], axis=0, keepdims=True))
        for out in (o1, o2, o3):
            out[ND + WHALF:, :] = packed


def relay(first, own_message, received, blocks):
    rows, width = own_message.shape
    out = jax.ShapeDtypeStruct((ND + rows - 3 * HALF, width), BF)
    return pl.pallas_call(
        functools.partial(relay_kernel, first, first),
        out_shape=(out,) * 3,
        in_specs=[VM] * 7,
        out_specs=(VM,) * 3,
        compiler_params=params(),
        name="relay",
    )(own_message, *received, *blocks)


def finish_kernel(scale, o00, xo, x1, x2, x3, yo, y1, y2, y3, weight, gfeat, wout, bout):
    total = o00[...].astype(F32)
    for ref in (x1, x2, x3, y1, y2, y3):
        total = total + ref[0:ND, :].astype(F32)
    gfeat[...] = lax.dot_general(
        total.astype(BF), weight[...], (((1,), (1,)), ((), ())), preferred_element_type=F32
    ).astype(BF)
    tops = sum4(*(ref[ND:, :].astype(F32) for ref in (xo, x1, x2, x3)))
    lows = sum4(*(ref[ND:, :].astype(F32) for ref in (yo, y1, y2, y3)))
    wout[0:WHALF, :] = tops[:WHALF] * scale
    wout[WHALF:, :] = lows * scale
    bout[...] = jnp.sum(tops[WHALF:], axis=0, keepdims=True) * scale


def finish(scale, o00, xs, ys, weight):
    width = o00.shape[1]
    return pl.pallas_call(
        functools.partial(finish_kernel, scale),
        out_shape=(
            jax.ShapeDtypeStruct((ND, width), BF),
            jax.ShapeDtypeStruct((WROWS, width), F32),
            jax.ShapeDtypeStruct((1, width), F32),
        ),
        in_specs=[VM] * 10,
        out_specs=(VM,) * 3,
        compiler_params=params(),
        name="finish",
    )(o00, *xs, *ys, weight)


def place_kernel(zpos, w0, w1, w2, w3, out):
    for dz, ref in enumerate((w0, w1, w2, w3)):
        start = pl.multiple_of(lax.rem(zpos[0] + SIDE - dz, SIDE) * WROWS, WROWS)
        out[pl.ds(start, WROWS), :] = ref[...]


def place(zpos, slices):
    width = slices[0].shape[1]
    return pl.pallas_call(
        place_kernel,
        out_shape=jax.ShapeDtypeStruct((SIDE * WROWS, width), F32),
        in_specs=[pl.BlockSpec(memory_space=pltpu.SMEM)] + [VM] * 4,
        out_specs=VM,
        compiler_params=params(),
        name="place",
    )(zpos, *slices)


def shards(features, weight, out_bias, cotangent, adj_tiles, tile_cols, tile_counts):
    row = lax.axis_index("row")
    col = lax.axis_index("col")
    x, y, z, k = row // SIDE, row % SIDE, col // 2, col % 2
    tile_rows = adj_tiles.shape[2]
    adj = adj_tiles.reshape(tile_rows, SLOTS, TILE, TILE)
    cols = tile_cols.reshape(tile_rows, SLOTS)
    source = cols // PER
    distance = (x - source // SIDE) % SIDE * SIDE + (y - source % SIDE) % SIDE
    live = lax.broadcasted_iota(jnp.int32, cols.shape, 1) < tile_counts.reshape(tile_rows, 1)
    index = jnp.where(live, distance * PER + cols % PER, DUMMY).reshape(-1)
    steps = jnp.arange(SIDE, dtype=jnp.int32)
    onward = (z + steps) % SIDE * 2
    back = (z - steps) % SIDE * 2
    order_forward = jnp.concatenate([onward + (1 - k), onward + k]).astype(jnp.int32)
    order_backward = jnp.concatenate([back + k, back + (1 - k)]).astype(jnp.int32)
    zpos = z.reshape(1).astype(jnp.int32)

    xs = [send_row(features, d, 0) for d in (1, 2, 3)]
    ys = [send_row(features, 0, d) for d in (1, 2, 3)]
    via_y = jnp.concatenate([v[:HALF] for v in xs], axis=0)
    via_x = jnp.concatenate([v[HALF:] for v in ys], axis=0)
    yb = [send_row(via_y, 0, d) for d in (1, 2, 3)]
    xb = [send_row(via_x, d, 0) for d in (1, 2, 3)]
    swap, keep = forward(order_forward, index, adj, [features, *xs, *ys, *yb, *xb])

    recv = send_col(swap, 0, 1)
    parts = []
    for d in (1, 2, 3):
        message = (keep[d].astype(F32) + recv[d].astype(F32)).astype(BF)
        parts.append(send_col(message, d, 0))
    activated, *messages = activation(zpos, keep, recv, parts, weight, out_bias.reshape(1, -1), cotangent)

    mine = [messages[0]] + [send_col(messages[d], d, 0) for d in (1, 2, 3)]
    theirs = [send_col(v, 0, 1) for v in mine]
    ym, xm, ox, oy, o00 = backward(order_backward, index, adj, mine + theirs)

    from_y = [send_row(ym[d - 1], 0, d) for d in (1, 2, 3)]
    from_x = [send_row(xm[d - 1], d, 0) for d in (1, 2, 3)]
    to_x = relay(True, ym[0], from_y, ox)
    to_y = relay(False, xm[0], from_x, oy)
    last_x = [send_row(to_x[d - 1], d, 0) for d in (1, 2, 3)]
    last_y = [send_row(to_y[d - 1], 0, d) for d in (1, 2, 3)]
    nodes = features.shape[0] * lax.axis_size("row") * lax.axis_size("col")
    grad_features, own_weight, grad_bias = finish(
        nodes**-0.5, o00, [to_x[0], *last_x], [to_y[0], *last_y], weight
    )
    slices = [own_weight] + [send_col(own_weight, d, 0) for d in (1, 2, 3)]
    grad_weight = place(zpos, slices)
    return activated, grad_features, grad_weight, grad_bias.reshape(-1)


def solution(mesh):
    in_specs = (
        P(("row", "col"), None),
        P(),
        P(),
        P(("row", "col"), None),
        P("row", "col", None, None, None, None),
        P("row", "col", None, None),
        P("row", "col", None),
    )
    out_specs = (P(("row", "col"), None), P(("row", "col"), None), P(), P())
    return jax.shard_map(shards, mesh=mesh, in_specs=in_specs, out_specs=out_specs, check_vma=False)
```

```python
import functools

import jax
import jax.numpy as jnp
from jax import lax
from jax.experimental import pallas as pl
from jax.experimental.pallas import tpu as pltpu
from jax.sharding import PartitionSpec as P


TILE = 128
SLOTS = 16
SIDE = 4
ND = 384
PER = ND // TILE
DUMMY = SIDE * SIDE * PER
BROWS = 16
BF = jnp.bfloat16
F32 = jnp.float32
VM = pl.BlockSpec(memory_space=pltpu.VMEM)


def send_plane(value, first, step):
    pairs = []
    for row in range(SIDE * SIDE):
        for col in range(2 * SIDE):
            x, y = divmod(row, SIDE)
            if (col % 2 == 0) == first:
                x = (x + step) % SIDE
            else:
                y = (y + step) % SIDE
            pairs.append((row * 2 * SIDE + col, (x * SIDE + y) * 2 * SIDE + col))
    return lax.ppermute(value, ("row", "col"), pairs)


def send_row(value, dx, dy):
    pairs = []
    for x in range(SIDE):
        for y in range(SIDE):
            pairs.append((x * SIDE + y, (x + dx) % SIDE * SIDE + (y + dy) % SIDE))
    return lax.ppermute(value, "row", pairs)


def send_col(value, dz, dk):
    pairs = []
    for z in range(SIDE):
        for k in range(2):
            pairs.append((z * 2 + k, (z + dz) % SIDE * 2 + (k ^ dk)))
    return lax.ppermute(value, "col", pairs)


def rel(first, second):
    return (second % SIDE) * SIDE + first % SIDE


def params(mb):
    return pltpu.CompilerParams(vmem_limit_bytes=mb * 1024 * 1024)


def cost(flops, data):
    return pl.CostEstimate(flops=flops, bytes_accessed=data, transcendentals=0)


def sum4(a, b, c, d):
    return (a + c) + (b + d)


def pack_bias(total):
    hi = total.astype(BF)
    lo = (total - hi.astype(F32)).astype(BF)
    rows = lax.broadcasted_iota(jnp.int32, (BROWS, total.shape[1]), 0)
    zero = jnp.zeros((BROWS, total.shape[1]), F32)
    return jnp.where(rows == 0, hi.astype(F32), jnp.where(rows == 1, lo.astype(F32), zero)).astype(BF)


def index_kernel(place, cols, counts, out):
    column = cols[...]
    source = (column * 43) >> 7
    away_x = (place[0] - (source >> 2)) & (SIDE - 1)
    away_y = (place[1] - source) & (SIDE - 1)
    distance = jnp.where(place[2] == 0, away_y * SIDE + away_x, away_x * SIDE + away_y)
    live = lax.broadcasted_iota(jnp.int32, column.shape, 1) < counts[...]
    out[...] = jnp.where(live, distance * PER + (column - source * PER), DUMMY)


def forward_rows(order, index, adj, panel, step, i):
    tile_row = order[step] * PER + i
    total = None
    for pair in range(SLOTS // 2):
        picked = []
        for half in range(2):
            start = pl.multiple_of(index[tile_row, 2 * pair + half] * TILE, TILE)
            picked.append(panel[pl.ds(start, TILE), :])
        left = jnp.concatenate([adj[i, 2 * pair], adj[i, 2 * pair + 1]], axis=1)
        product = jnp.dot(left, jnp.concatenate(picked, axis=0), preferred_element_type=F32)
        total = product if total is None else total + product
    return total.astype(BF)


def forward_first_kernel(order, index, adj, own, f1, f2, f3, s1, s2, s3, m1, m2, m3, out, panel):
    step = pl.program_id(0)

    @pl.when(step == 0)
    def _():
        panel[0:ND, :] = own[...]
        for a, ref in enumerate((f1, f2, f3)):
            panel[rel(a + 1, 0) * ND:(rel(a + 1, 0) + 1) * ND, :] = ref[...]
        for b, (side, many) in enumerate(((s1, m1), (s2, m2), (s3, m3))):
            start = rel(0, b + 1) * ND
            panel[start:start + ND, :] = side[...]
            panel[start + ND:start + SIDE * ND, :] = many[...]
        panel[DUMMY * TILE:, :] = jnp.zeros((TILE, panel.shape[1]), BF)

    for i in range(PER):
        out[step, i * TILE:(i + 1) * TILE, :] = forward_rows(order, index, adj, panel, step, i)


def forward_next_kernel(offset, order, index, adj, panel, out):
    step = pl.program_id(0)
    for i in range(PER):
        out[step, i * TILE:(i + 1) * TILE, :] = forward_rows(order, index, adj, panel, step + offset, i)


def forward(offset, steps, order, index, adj, operands):
    width = operands[0].shape[1]
    first = len(operands) > 1
    shape = jax.ShapeDtypeStruct((steps, ND, width), BF)
    panel = jax.ShapeDtypeStruct(((DUMMY + 1) * TILE, width), BF)
    return pl.pallas_call(
        forward_first_kernel if first else functools.partial(forward_next_kernel, offset),
        out_shape=(shape, panel) if first else shape,
        grid_spec=pltpu.PrefetchScalarGridSpec(
            num_scalar_prefetch=2,
            grid=(steps,),
            in_specs=[pl.BlockSpec((PER, SLOTS, TILE, TILE), lambda s, o, n: (o[s + offset], 0, 0, 0))]
            + [VM] * len(operands),
            out_specs=(VM, VM) if first else VM,
        ),
        compiler_params=params(12),
        cost_estimate=cost(steps * PER * SLOTS * 2 * TILE * TILE * width, steps * PER * SLOTS * TILE * TILE * 2),
        name="forward",
    )(order, index, adj, *operands)


def activation_kernel(keep, recv, r1, r2, r3, weight, bias, cot, act, grad_out, terms):
    agg = keep[0].astype(F32) + recv[0].astype(F32)
    for ref in (r1, r2, r3):
        agg = agg + ref[...].astype(F32)
    agg16 = agg.astype(BF)
    pre = jnp.dot(agg16, weight[...], preferred_element_type=F32) + bias[...]
    sig = 1.0 / (1.0 + jnp.exp(-pre))
    act[...] = (pre * sig).astype(BF)
    grad = (cot[...].astype(F32) * sig * (1.0 + pre * (1.0 - sig))).astype(BF)
    grad_out[...] = grad
    wrows = terms.shape[0] - BROWS
    terms[0:wrows, :] = lax.dot_general(
        agg16, grad, (((0,), (0,)), ((), ())), preferred_element_type=F32
    ).astype(BF)
    terms[wrows:, :] = pack_bias(jnp.sum(grad.astype(F32), axis=0, keepdims=True))


def backward_kernel(offset, count, initial, final, order, index, adj, *refs):
    sources, refs = refs[:count], refs[count:]
    if not initial:
        refs = refs[1:]
    acc, refs = refs[0], refs[1:]
    if final:
        own, sides, many = refs[0], refs[1:SIDE], refs[SIDE:2 * SIDE - 1]
    turned = refs[-1]
    step = pl.program_id(0)

    @pl.when(step == 0)
    def _():
        for s, ref in enumerate(sources):
            for i in range(PER):
                turned[s * PER + i] = ref[i * TILE:(i + 1) * TILE, :].T
        if initial:
            acc[...] = jnp.zeros_like(acc)

    for i in range(PER):
        tile_row = order[step + offset] * PER + i
        left = turned[step * PER + i]
        for pair in range(SLOTS // 2):
            right = jnp.concatenate([adj[i, 2 * pair], adj[i, 2 * pair + 1]], axis=1)
            product = jnp.dot(left, right, preferred_element_type=F32)
            first = index[tile_row, 2 * pair]
            second = index[tile_row, 2 * pair + 1]
            acc[first] = acc[first] + product[:, :TILE]
            acc[second] = acc[second] + product[:, TILE:]

    if final:
        @pl.when(step == count - 1)
        def _():
            for b in (1, 2, 3, 0):
                for a in range(SIDE):
                    if b == 0:
                        out, start = own, a * ND
                    elif a == 0:
                        out, start = sides[b - 1], 0
                    else:
                        out, start = many[b - 1], (a - 1) * ND
                    for n in range(PER):
                        row = start + n * TILE
                        out[row:row + TILE, :] = acc[rel(-a, -b) * PER + n].astype(BF).T


def backward(offset, order, index, adj, sources, acc=None, final=False):
    width = sources[0].shape[1]
    count = len(sources)
    state = jax.ShapeDtypeStruct((DUMMY + 1, width, TILE), F32)
    outs = (state,)
    if final:
        outs += tuple(jax.ShapeDtypeStruct((n * ND, width), BF) for n in (SIDE, 1, 1, 1, 3, 3, 3))
    initial = acc is None
    extra = [] if initial else [acc]
    return pl.pallas_call(
        functools.partial(backward_kernel, offset, count, initial, final),
        out_shape=outs,
        grid_spec=pltpu.PrefetchScalarGridSpec(
            num_scalar_prefetch=2,
            grid=(count,),
            in_specs=[pl.BlockSpec((PER, SLOTS, TILE, TILE), lambda s, o, n: (o[s + offset], 0, 0, 0))]
            + [VM] * (count + len(extra)),
            out_specs=[VM] * len(outs),
            scratch_shapes=[pltpu.VMEM((count * PER, width, TILE), BF)],
        ),
        input_output_aliases={} if initial else {3 + count: 0},
        compiler_params=params(16),
        cost_estimate=cost(count * PER * SLOTS * 2 * TILE * TILE * width, count * PER * SLOTS * TILE * TILE * 2),
        name="backward",
    )(order, index, adj, *sources, *extra)


def add_terms_kernel(t0, t1, t2, t3, out):
    total = sum4(*(ref[...].astype(F32) for ref in (t0, t1, t2, t3)))
    wrows = out.shape[0] - BROWS
    out[0:wrows, :] = total[:wrows].astype(BF)
    out[wrows:, :] = pack_bias(jnp.sum(total[wrows:], axis=0, keepdims=True))


def last_terms_kernel(scale, t0, t1, wout, bout):
    total = t0[...].astype(F32) + t1[...].astype(F32)
    wrows = wout.shape[0]
    wout[...] = total[:wrows] * scale
    bout[...] = jnp.sum(total[wrows:], axis=0, keepdims=True) * scale


def small(kernel, outs, operands):
    return pl.pallas_call(
        kernel,
        out_shape=outs,
        in_specs=[VM] * len(operands),
        out_specs=jax.tree.map(lambda _: VM, outs),
        compiler_params=params(8),
    )(*operands)


def relay_kernel(own, r1, r2, r3, *outs):
    for a, out in enumerate(outs):
        total = own[(a + 1) * ND:(a + 2) * ND, :].astype(F32)
        for ref in (r1, r2, r3):
            total = total + ref[a * ND:(a + 1) * ND, :].astype(F32)
        out[...] = total.astype(BF)


def finish_kernel(own, *refs):
    weight, gfeat = refs[-2:]
    total = own[0:ND, :].astype(F32)
    for ref in refs[:-2]:
        total = total + ref[...].astype(F32)
    gfeat[...] = lax.dot_general(
        total.astype(BF), weight[...], (((1,), (1,)), ((), ())), preferred_element_type=F32
    ).astype(BF)


def shards(features, weight, out_bias, cotangent, adj_tiles, tile_cols, tile_counts):
    row = lax.axis_index("row")
    col = lax.axis_index("col")
    x, y, z, k = row // SIDE, row % SIDE, col // 2, col % 2
    width = features.shape[1]
    tile_rows = adj_tiles.shape[2]
    adj = pltpu.with_memory_space_constraint(adj_tiles.reshape(tile_rows, SLOTS, TILE, TILE), pltpu.HBM)
    place = jnp.stack([x, y, k]).astype(jnp.int32)
    index = pl.pallas_call(
        index_kernel,
        out_shape=jax.ShapeDtypeStruct((tile_rows, SLOTS), jnp.int32),
        in_specs=[pl.BlockSpec(memory_space=pltpu.SMEM), VM, VM],
        out_specs=VM,
        compiler_params=params(4),
        name="index",
    )(place, tile_cols.reshape(tile_rows, SLOTS), tile_counts.reshape(tile_rows, 1))
    other = 1 - k
    onward = [(z + d) % SIDE * 2 for d in range(SIDE)]
    back = [(z - d) % SIDE * 2 for d in range(SIDE)]
    order_forward = jnp.stack(
        [v + other for v in onward] + [v + k for v in onward[1:]] + [onward[0] + k]
    ).astype(jnp.int32)
    order_backward = jnp.stack(
        [back[0] + k, back[0] + other] + [v + k for v in back[1:]] + [v + other for v in back[1:]]
    ).astype(jnp.int32)

    def fan(send, values):
        received = []
        for d in (1, 2, 3):
            received.append(send(values[d - 1], d))
        return received

    first = fan(lambda v, d: send_plane(v, True, d), [features] * 3)
    side = fan(lambda v, d: send_plane(v, False, d), [features] * 3)
    line = jnp.concatenate(first, axis=0)
    many = fan(lambda v, d: send_plane(v, False, d), [line] * 3)
    swap, panel = forward(0, SIDE, order_forward, index, adj, [features, *first, *side, *many])

    recv = send_col(swap, 0, 1)
    away = forward(SIDE, SIDE - 1, order_forward, index, adj, [panel])
    messages = [(away[d - 1].astype(F32) + recv[d].astype(F32)).astype(BF) for d in (1, 2, 3)]
    parts = fan(lambda v, d: send_col(v, d, 0), messages)
    keep = forward(2 * SIDE - 1, 1, order_forward, index, adj, [panel])
    block = jax.ShapeDtypeStruct((ND, width), BF)
    terms = jax.ShapeDtypeStruct((width + BROWS, width), BF)
    activated, grad, along = small(
        activation_kernel, (block, block, terms), [keep, recv, *parts, weight, out_bias.reshape(1, -1), cotangent]
    )

    mine = [grad] + fan(lambda v, d: send_col(v, d, 0), [grad] * 3)
    theirs = [send_col(grad, 0, 1)]
    theirs += fan(lambda v, d: send_col(v, 0, 1), mine[1:])
    along_x = [along] + fan(lambda v, d: send_row(v, d, 0), [along] * 3)
    acc, = backward(0, order_backward, index, adj, [mine[0], theirs[0]])
    along = small(add_terms_kernel, terms, along_x)
    along_y = [along] + fan(lambda v, d: send_row(v, 0, d), [along] * 3)
    acc, = backward(2, order_backward, index, adj, mine[1:], acc)
    acc, own, *blocks = backward(SIDE + 1, order_backward, index, adj, theirs[1:], acc, final=True)

    landed = fan(lambda v, d: send_plane(v, False, d), blocks[3:])
    beside = fan(lambda v, d: send_plane(v, False, d), blocks[:3])
    along = small(add_terms_kernel, terms, along_y)
    along_z = [along] + fan(lambda v, d: send_col(v, d, 0), [along] * 3)
    along = small(add_terms_kernel, terms, along_z)
    partner = send_col(along, 0, 1)
    nodes = features.shape[0] * lax.axis_size("row") * lax.axis_size("col")
    grad_weight, grad_bias = small(
        functools.partial(last_terms_kernel, nodes**-0.5),
        (jax.ShapeDtypeStruct((width, width), F32), jax.ShapeDtypeStruct((1, width), F32)),
        [along, partner],
    )
    onwards = small(relay_kernel, (block,) * 3, [own, *landed])
    last = fan(lambda v, d: send_plane(v, True, d), onwards)
    grad_features = small(finish_kernel, block, [own, *last, *beside, weight])
    return activated, grad_features, grad_weight, grad_bias.reshape(-1)


def solution(mesh):
    in_specs = (
        P(("row", "col"), None),
        P(),
        P(),
        P(("row", "col"), None),
        P("row", "col", None, None, None, None),
        P("row", "col", None, None),
        P("row", "col", None),
    )
    out_specs = (P(("row", "col"), None), P(("row", "col"), None), P(), P())

    return jax.shard_map(shards, mesh=mesh, in_specs=in_specs, out_specs=out_specs, check_vma=False)
```

```python
import functools

import jax
import jax.numpy as jnp
from jax import lax
from jax.experimental import pallas as pl
from jax.experimental.pallas import tpu as pltpu
from jax.sharding import PartitionSpec as P


TILE = 128
SLOTS = 16
SIDE = 4
ND = 384
PER = ND // TILE
DUMMY = SIDE * SIDE * PER
BROWS = 16
BF = jnp.bfloat16
F32 = jnp.float32
VM = pl.BlockSpec(memory_space=pltpu.VMEM)
SM = pl.BlockSpec(memory_space=pltpu.SMEM)


def send_plane(value, first, step):
    pairs = []
    for row in range(SIDE * SIDE):
        for col in range(2 * SIDE):
            x, y = divmod(row, SIDE)
            if (col % 2 == 0) == first:
                x = (x + step) % SIDE
            else:
                y = (y + step) % SIDE
            pairs.append((row * 2 * SIDE + col, (x * SIDE + y) * 2 * SIDE + col))
    return lax.ppermute(value, ("row", "col"), pairs)


def trade_row(value, bit, along_x):
    pairs = []
    for x in range(SIDE):
        for y in range(SIDE):
            there = ((x ^ bit), y) if along_x else (x, (y ^ bit))
            pairs.append((x * SIDE + y, there[0] * SIDE + there[1]))
    return lax.ppermute(value, "row", pairs)


def send_col(value, dz, dk):
    pairs = []
    for z in range(SIDE):
        for k in range(2):
            pairs.append((z * 2 + k, (z + dz) % SIDE * 2 + (k ^ dk)))
    return lax.ppermute(value, "col", pairs)


def rel(first, second):
    return (second % SIDE) * SIDE + first % SIDE


def params(mb):
    return pltpu.CompilerParams(vmem_limit_bytes=mb * 1024 * 1024)


def cost(flops, data):
    return pl.CostEstimate(flops=flops, bytes_accessed=data, transcendentals=0)


def sum4(a, b, c, d):
    return (a + c) + (b + d)


def pack_bias(total):
    hi = total.astype(BF)
    lo = (total - hi.astype(F32)).astype(BF)
    rows = lax.broadcasted_iota(jnp.int32, (BROWS, total.shape[1]), 0)
    zero = jnp.zeros((BROWS, total.shape[1]), F32)
    return jnp.where(rows == 0, hi.astype(F32), jnp.where(rows == 1, lo.astype(F32), zero)).astype(BF)


def mark_kernel(out):
    out[...] = jnp.zeros_like(out)


def join_kernel(*refs):
    for n, ref in enumerate(refs[:-1]):
        refs[-1][n * ND:(n + 1) * ND, :] = ref[...]


def load_kernel(source, out, sems):
    parts = sems.shape[0]
    chunk = source.shape[0] // parts
    copies = []
    for n in range(parts):
        part = pl.ds(n * chunk, chunk)
        copies.append(pltpu.make_async_copy(source.at[part], out.at[part], sems.at[n]))
    for n in range(parts + 2):
        if n < parts:
            copies[n].start()
        if n >= 2:
            copies[n - 2].wait()


def index_kernel(place, cols, counts, mark, out):
    column = cols[...]
    source = (column * 43) >> 7
    away_x = (place[0] - (source >> 2)) & (SIDE - 1)
    away_y = (place[1] - source) & (SIDE - 1)
    distance = jnp.where(place[2] == 0, away_y * SIDE + away_x, away_x * SIDE + away_y)
    live = lax.broadcasted_iota(jnp.int32, column.shape, 1) < counts[...]
    out[...] = jnp.where(live, distance * PER + (column - source * PER), DUMMY) + mark[0:1, 0:1]


def forward_steps(offset, steps, order, index, adj, panel, out):
    def body(step, carry):
        for i in range(PER):
            tile_row = order[step + offset] * PER + i
            total = None
            for pair in range(SLOTS // 2):
                picked = []
                for half in range(2):
                    start = pl.multiple_of(index[tile_row, 2 * pair + half] * TILE, TILE)
                    picked.append(panel[pl.ds(start, TILE), :])
                left = jnp.concatenate([adj[tile_row, 2 * pair], adj[tile_row, 2 * pair + 1]], axis=1)
                product = jnp.dot(left, jnp.concatenate(picked, axis=0), preferred_element_type=F32)
                total = product if total is None else total + product
            out[step, i * TILE:(i + 1) * TILE, :] = total.astype(BF)
        return carry

    lax.fori_loop(0, steps, body, 0)


def forward_first_kernel(offset, steps, order, index, adj, own, f1, f2, f3, s1, s2, s3, m1, m2, m3, out, panel):
    panel[0:ND, :] = own[...]
    for a, ref in enumerate((f1, f2, f3)):
        panel[rel(a + 1, 0) * ND:(rel(a + 1, 0) + 1) * ND, :] = ref[...]
    for b, (side, many) in enumerate(((s1, m1), (s2, m2), (s3, m3))):
        start = rel(0, b + 1) * ND
        panel[start:start + ND, :] = side[...]
        panel[start + ND:start + SIDE * ND, :] = many[...]
    panel[DUMMY * TILE:, :] = jnp.zeros((TILE, panel.shape[1]), BF)
    forward_steps(offset, steps, order, index, adj, panel, out)


def forward(offset, steps, order, index, adj, operands):
    width = operands[0].shape[1]
    first = len(operands) > 1
    shape = jax.ShapeDtypeStruct((steps, ND, width), BF)
    panel = jax.ShapeDtypeStruct(((DUMMY + 1) * TILE, width), BF)
    return pl.pallas_call(
        functools.partial(forward_first_kernel if first else forward_steps, offset, steps),
        out_shape=(shape, panel) if first else shape,
        in_specs=[SM, SM] + [VM] * (1 + len(operands)),
        out_specs=(VM, VM) if first else VM,
        compiler_params=params(6),
        cost_estimate=cost(steps * PER * SLOTS * 2 * TILE * TILE * width, steps * PER * SLOTS * TILE * TILE * 2),
    )(order, index, adj, *operands)


def activation_kernel(keep, recv, r1, r2, r3, weight, bias, cot, act, grad_out, terms):
    agg = keep[1].astype(F32) + recv[...].astype(F32)
    for ref in (r1, r2, r3):
        agg = agg + ref[...].astype(F32)
    agg16 = agg.astype(BF)
    pre = jnp.dot(agg16, weight[...], preferred_element_type=F32) + bias[...]
    sig = 1.0 / (1.0 + jnp.exp(-pre))
    act[...] = (pre * sig).astype(BF)
    grad = (cot[...].astype(F32) * sig * (1.0 + pre * (1.0 - sig))).astype(BF)
    grad_out[...] = grad
    wrows = terms.shape[0] - BROWS
    terms[0:wrows, :] = lax.dot_general(
        agg16, grad, (((0,), (0,)), ((), ())), preferred_element_type=F32
    ).astype(BF)
    terms[wrows:, :] = pack_bias(jnp.sum(grad.astype(F32), axis=0, keepdims=True))


def backward_kernel(offset, count, initial, final, order, index, adj, *refs):
    sources, refs = refs[:count], refs[count:]
    if not initial:
        refs = refs[1:]
    acc, refs = refs[0], refs[1:]
    if final:
        own, sides, many = refs[0], refs[1:SIDE], refs[SIDE:2 * SIDE - 1]
    turned, tiles, sems = refs[-3:]

    def fetch(step):
        rows = pl.ds(order[step + offset] * PER, PER)
        return pltpu.make_async_copy(adj.at[rows], tiles.at[step], sems.at[step])

    for step in range(count):
        fetch(step).start()
    for s, ref in enumerate(sources):
        for i in range(PER):
            turned[s * PER + i] = ref[i * TILE:(i + 1) * TILE, :].T
    if initial:
        acc[...] = jnp.zeros_like(acc)

    def body(step, carry):
        fetch(step).wait()
        for i in range(PER):
            tile_row = order[step + offset] * PER + i
            left = turned[step * PER + i]
            for slot in range(SLOTS):
                product = jnp.dot(left, tiles[step, i, slot], preferred_element_type=F32)
                place = index[tile_row, slot]
                acc[place] = acc[place] + product
        return carry

    lax.fori_loop(0, count, body, 0)

    if final:
        for b in (1, 2, 3, 0):
            for a in range(SIDE):
                if b == 0:
                    out, start = own, a * ND
                elif a == 0:
                    out, start = sides[b - 1], 0
                else:
                    out, start = many[b - 1], (a - 1) * ND
                for n in range(PER):
                    row = start + n * TILE
                    out[row:row + TILE, :] = acc[rel(-a, -b) * PER + n].astype(BF).T


def backward(offset, order, index, adj, sources, acc=None, final=False):
    width = sources[0].shape[1]
    count = len(sources)
    state = jax.ShapeDtypeStruct((DUMMY + 1, width, TILE), F32)
    outs = (state,)
    if final:
        outs += tuple(jax.ShapeDtypeStruct((n * ND, width), BF) for n in (SIDE, 1, 1, 1, 3, 3, 3))
    initial = acc is None
    extra = [] if initial else [acc]
    return pl.pallas_call(
        functools.partial(backward_kernel, offset, count, initial, final),
        out_shape=outs,
        in_specs=[SM, SM, pl.BlockSpec(memory_space=pltpu.HBM)] + [VM] * (count + len(extra)),
        out_specs=[VM] * len(outs),
        scratch_shapes=[
            pltpu.VMEM((count * PER, width, TILE), BF),
            pltpu.VMEM((count, PER, SLOTS, TILE, TILE), BF),
            pltpu.SemaphoreType.DMA((count,)),
        ],
        input_output_aliases={} if initial else {3 + count: 0},
        compiler_params=params(8),
        cost_estimate=cost(count * PER * SLOTS * 2 * TILE * TILE * width, count * PER * SLOTS * TILE * TILE * 2),
    )(order, index, adj, *sources, *extra)


def add_terms_kernel(*refs):
    terms, out = [ref[...].astype(F32) for ref in refs[:-1]], refs[-1]
    total = sum4(*terms) if len(terms) == SIDE else terms[0] + terms[1]
    wrows = out.shape[0] - BROWS
    out[0:wrows, :] = total[:wrows].astype(BF)
    out[wrows:, :] = pack_bias(jnp.sum(total[wrows:], axis=0, keepdims=True))


def last_terms_kernel(scale, t0, t1, wout, bout):
    total = t0[...].astype(F32) + t1[...].astype(F32)
    wrows = wout.shape[0]
    wout[...] = total[:wrows] * scale
    bout[...] = jnp.sum(total[wrows:], axis=0, keepdims=True) * scale


def small(kernel, outs, operands):
    return pl.pallas_call(
        kernel,
        out_shape=outs,
        in_specs=[VM] * len(operands),
        out_specs=jax.tree.map(lambda _: VM, outs),
        compiler_params=params(8),
    )(*operands)


def relay_kernel(own, r1, r2, r3, *outs):
    for a, out in enumerate(outs):
        total = own[(a + 1) * ND:(a + 2) * ND, :].astype(F32)
        for ref in (r1, r2, r3):
            total = total + ref[a * ND:(a + 1) * ND, :].astype(F32)
        out[...] = total.astype(BF)


def finish_kernel(own, *refs):
    weight, gfeat = refs[-2:]
    total = own[0:ND, :].astype(F32)
    for ref in refs[:-2]:
        total = total + ref[...].astype(F32)
    gfeat[...] = lax.dot_general(
        total.astype(BF), weight[...], (((1,), (1,)), ((), ())), preferred_element_type=F32
    ).astype(BF)


def shards(features, weight, out_bias, cotangent, adj_tiles, tile_cols, tile_counts):
    row = lax.axis_index("row")
    col = lax.axis_index("col")
    x, y, z, k = row // SIDE, row % SIDE, col // 2, col % 2
    width = features.shape[1]
    tile_rows = adj_tiles.shape[2]
    adj = pltpu.with_memory_space_constraint(adj_tiles.reshape(tile_rows, SLOTS, TILE, TILE), pltpu.HBM)
    mark = small(mark_kernel, jax.ShapeDtypeStruct((8, 128), jnp.int32), [])
    place = jnp.stack([x, y, k]).astype(jnp.int32)
    index = pl.pallas_call(
        index_kernel,
        out_shape=jax.ShapeDtypeStruct((tile_rows, SLOTS), jnp.int32),
        in_specs=[SM, VM, VM, VM],
        out_specs=VM,
        compiler_params=params(1),
    )(place, tile_cols.reshape(tile_rows, SLOTS), tile_counts.reshape(tile_rows, 1), mark)
    held = pl.pallas_call(
        load_kernel,
        out_shape=jax.ShapeDtypeStruct(adj.shape, adj.dtype),
        in_specs=[pl.BlockSpec(memory_space=pltpu.HBM)],
        out_specs=VM,
        scratch_shapes=[pltpu.SemaphoreType.DMA((12,))],
        compiler_params=params(1),
    )(adj)
    other = 1 - k
    onward = [(z + d) % SIDE * 2 for d in range(SIDE)]
    back = [(z - d) % SIDE * 2 for d in range(SIDE)]
    order_forward = jnp.stack(
        [v + other for v in onward[1:]] + [v + k for v in onward[1:]] + [onward[0] + other, onward[0] + k]
    ).astype(jnp.int32)
    order_backward = jnp.stack(
        [back[0] + k, back[0] + other] + [v + k for v in back[1:]] + [v + other for v in back[1:]]
    ).astype(jnp.int32)

    def fan(send, values):
        received = []
        for d in (1, 2, 3):
            received.append(send(values[d - 1], d))
        return received

    first = fan(lambda v, d: send_plane(v, True, d), [features] * 3)
    side = fan(lambda v, d: send_plane(v, False, d), [features] * 3)
    line = small(join_kernel, jax.ShapeDtypeStruct((3 * ND, width), BF), first)
    many = fan(lambda v, d: send_plane(v, False, d), [line] * 3)
    swap, panel = forward(0, 3, order_forward, index, held, [features, *first, *side, *many])

    recv = send_col(swap, 0, 1)
    away = forward(3, 3, order_forward, index, held, [panel])
    messages = [(away[d].astype(F32) + recv[d].astype(F32)).astype(BF) for d in range(3)]
    parts = fan(lambda v, d: send_col(v, d, 0), messages)
    keep = forward(6, 2, order_forward, index, held, [panel])
    recv = send_col(keep[0], 0, 1)
    block = jax.ShapeDtypeStruct((ND, width), BF)
    terms = jax.ShapeDtypeStruct((width + BROWS, width), BF)
    activated, grad, along = small(
        activation_kernel,
        (block, block, terms),
        [keep, recv, *parts, weight, out_bias.reshape(1, -1), cotangent],
    )

    mine = [grad] + fan(lambda v, d: send_col(v, d, 0), [grad] * 3)
    theirs = [send_col(grad, 0, 1)]
    theirs += fan(lambda v, d: send_col(v, 0, 1), mine[1:])
    other_terms = trade_row(along, 1, True)
    acc, = backward(0, order_backward, index, adj, [mine[0], theirs[0]])
    along = small(add_terms_kernel, terms, [along, other_terms])
    other_terms = trade_row(along, 2, True)
    acc, = backward(2, order_backward, index, adj, mine[1:], acc)
    along = small(add_terms_kernel, terms, [along, other_terms])
    other_terms = trade_row(along, 1, False)
    acc, own, *blocks = backward(SIDE + 1, order_backward, index, adj, theirs[1:], acc, final=True)

    landed = fan(lambda v, d: send_plane(v, False, d), blocks[3:])
    beside = fan(lambda v, d: send_plane(v, False, d), blocks[:3])
    along = small(add_terms_kernel, terms, [along, other_terms])
    along_z = [along] + fan(lambda v, d: send_col(v, d, 0), [along] * 3)
    along = small(add_terms_kernel, terms, along_z)
    other_terms = send_col(along, 0, 1)
    along = small(add_terms_kernel, terms, [along, other_terms])
    other_terms = trade_row(along, 2, False)
    nodes = features.shape[0] * lax.axis_size("row") * lax.axis_size("col")
    grad_weight, grad_bias = small(
        functools.partial(last_terms_kernel, nodes**-0.5),
        (jax.ShapeDtypeStruct((width, width), F32), jax.ShapeDtypeStruct((1, width), F32)),
        [along, other_terms],
    )
    onwards = small(relay_kernel, (block,) * 3, [own, *landed])
    last = fan(lambda v, d: send_plane(v, True, d), onwards)
    grad_features = small(finish_kernel, block, [own, *last, *beside, weight])
    return activated, grad_features, grad_weight, grad_bias.reshape(-1)


def solution(mesh):
    in_specs = (
        P(("row", "col"), None),
        P(),
        P(),
        P(("row", "col"), None),
        P("row", "col", None, None, None, None),
        P("row", "col", None, None),
        P("row", "col", None),
    )
    out_specs = (P(("row", "col"), None), P(("row", "col"), None), P(), P())

    return jax.shard_map(shards, mesh=mesh, in_specs=in_specs, out_specs=out_specs, check_vma=False)
```

```python
import functools

import jax
import jax.numpy as jnp
from jax import lax
from jax.experimental import pallas as pl
from jax.experimental.pallas import tpu as pltpu
from jax.sharding import PartitionSpec as P


TILE = 128
SLOTS = 16
SIDE = 4
ND = 384
PER = ND // TILE
DUMMY = SIDE * SIDE * PER
BROWS = 16
BF = jnp.bfloat16
F32 = jnp.float32
VM = pl.BlockSpec(memory_space=pltpu.VMEM)
SM = pl.BlockSpec(memory_space=pltpu.SMEM)


def send_plane(value, first, step):
    pairs = []
    for row in range(SIDE * SIDE):
        for col in range(2 * SIDE):
            x, y = divmod(row, SIDE)
            if (col % 2 == 0) == first:
                x = (x + step) % SIDE
            else:
                y = (y + step) % SIDE
            pairs.append((row * 2 * SIDE + col, (x * SIDE + y) * 2 * SIDE + col))
    return lax.ppermute(value, ("row", "col"), pairs)


def trade_row(value, bit, along_x):
    pairs = []
    for x in range(SIDE):
        for y in range(SIDE):
            there = ((x ^ bit), y) if along_x else (x, (y ^ bit))
            pairs.append((x * SIDE + y, there[0] * SIDE + there[1]))
    return lax.ppermute(value, "row", pairs)


def send_col(value, dz, dk):
    pairs = []
    for z in range(SIDE):
        for k in range(2):
            pairs.append((z * 2 + k, (z + dz) % SIDE * 2 + (k ^ dk)))
    return lax.ppermute(value, "col", pairs)


def rel(first, second):
    return (second % SIDE) * SIDE + first % SIDE


def params(mb):
    return pltpu.CompilerParams(vmem_limit_bytes=mb * 1024 * 1024)


def cost(flops, data):
    return pl.CostEstimate(flops=flops, bytes_accessed=data, transcendentals=0)


def sum4(a, b, c, d):
    return (a + c) + (b + d)


def pack_bias(total):
    hi = total.astype(BF)
    lo = (total - hi.astype(F32)).astype(BF)
    rows = lax.broadcasted_iota(jnp.int32, (BROWS, total.shape[1]), 0)
    zero = jnp.zeros((BROWS, total.shape[1]), F32)
    return jnp.where(rows == 0, hi.astype(F32), jnp.where(rows == 1, lo.astype(F32), zero)).astype(BF)


def mark_kernel(out):
    out[...] = jnp.zeros_like(out)


def join_kernel(*refs):
    for n, ref in enumerate(refs[:-1]):
        refs[-1][n * ND:(n + 1) * ND, :] = ref[...]


def load_kernel(source, out, sems):
    parts = sems.shape[0]
    chunk = source.shape[0] // parts
    copies = []
    for n in range(parts):
        part = pl.ds(n * chunk, chunk)
        copies.append(pltpu.make_async_copy(source.at[part], out.at[part], sems.at[n]))
    for n in range(parts + 2):
        if n < parts:
            copies[n].start()
        if n >= 2:
            copies[n - 2].wait()


def index_kernel(place, cols, counts, mark, out):
    column = cols[...]
    source = (column * 43) >> 7
    away_x = (place[0] - (source >> 2)) & (SIDE - 1)
    away_y = (place[1] - source) & (SIDE - 1)
    distance = jnp.where(place[2] == 0, away_y * SIDE + away_x, away_x * SIDE + away_y)
    live = lax.broadcasted_iota(jnp.int32, column.shape, 1) < counts[...]
    out[...] = jnp.where(live, distance * PER + (column - source * PER), DUMMY) + mark[0:1, 0:1]


def forward_steps(offset, steps, order, index, adj, panel, out):
    def body(step, carry):
        for i in range(PER):
            tile_row = order[step + offset] * PER + i
            total = None
            for pair in range(SLOTS // 2):
                picked = []
                for half in range(2):
                    start = pl.multiple_of(index[tile_row, 2 * pair + half] * TILE, TILE)
                    picked.append(panel[pl.ds(start, TILE), :])
                left = jnp.concatenate([adj[tile_row, 2 * pair], adj[tile_row, 2 * pair + 1]], axis=1)
                product = jnp.dot(left, jnp.concatenate(picked, axis=0), preferred_element_type=F32)
                total = product if total is None else total + product
            out[step, i * TILE:(i + 1) * TILE, :] = total.astype(BF)
        return carry

    lax.fori_loop(0, steps, body, 0)


def forward_first_kernel(offset, steps, order, index, adj, own, f1, f2, f3, s1, s2, s3, m1, m2, m3, out, panel):
    panel[0:ND, :] = own[...]
    for a, ref in enumerate((f1, f2, f3)):
        panel[rel(a + 1, 0) * ND:(rel(a + 1, 0) + 1) * ND, :] = ref[...]
    for b, (side, many) in enumerate(((s1, m1), (s2, m2), (s3, m3))):
        start = rel(0, b + 1) * ND
        panel[start:start + ND, :] = side[...]
        panel[start + ND:start + SIDE * ND, :] = many[...]
    panel[DUMMY * TILE:, :] = jnp.zeros((TILE, panel.shape[1]), BF)
    forward_steps(offset, steps, order, index, adj, panel, out)


def forward(offset, steps, order, index, adj, operands):
    width = operands[0].shape[1]
    first = len(operands) > 1
    shape = jax.ShapeDtypeStruct((steps, ND, width), BF)
    panel = jax.ShapeDtypeStruct(((DUMMY + 1) * TILE, width), BF)
    return pl.pallas_call(
        functools.partial(forward_first_kernel if first else forward_steps, offset, steps),
        out_shape=(shape, panel) if first else shape,
        in_specs=[SM, SM] + [VM] * (1 + len(operands)),
        out_specs=(VM, VM) if first else VM,
        compiler_params=params(6),
        cost_estimate=cost(steps * PER * SLOTS * 2 * TILE * TILE * width, steps * PER * SLOTS * TILE * TILE * 2),
    )(order, index, adj, *operands)


def activation_kernel(keep, recv, r1, r2, r3, weight, bias, cot, act, grad_out, terms):
    agg = keep[1].astype(F32) + recv[...].astype(F32)
    for ref in (r1, r2, r3):
        agg = agg + ref[...].astype(F32)
    agg16 = agg.astype(BF)
    pre = jnp.dot(agg16, weight[...], preferred_element_type=F32) + bias[...]
    sig = 1.0 / (1.0 + jnp.exp(-pre))
    act[...] = (pre * sig).astype(BF)
    grad = (cot[...].astype(F32) * sig * (1.0 + pre * (1.0 - sig))).astype(BF)
    grad_out[...] = grad
    wrows = terms.shape[0] - BROWS
    terms[0:wrows, :] = lax.dot_general(
        agg16, grad, (((0,), (0,)), ((), ())), preferred_element_type=F32
    ).astype(BF)
    terms[wrows:, :] = pack_bias(jnp.sum(grad.astype(F32), axis=0, keepdims=True))


def backward_kernel(offset, count, initial, final, order, index, adj, *refs):
    sources, refs = refs[:count], refs[count:]
    if not initial:
        refs = refs[1:]
    acc, refs = refs[0], refs[1:]
    if final:
        many = refs[:3]
    turned, tiles, sems = refs[-3:]

    def fetch(step):
        rows = pl.ds(order[step + offset] * PER, PER)
        return pltpu.make_async_copy(adj.at[rows], tiles.at[step], sems.at[step])

    for step in range(count):
        fetch(step).start()
    for s, ref in enumerate(sources):
        for i in range(PER):
            turned[s * PER + i] = ref[i * TILE:(i + 1) * TILE, :].T
    if initial:
        acc[...] = jnp.zeros_like(acc)

    def body(step, carry):
        fetch(step).wait()
        for i in range(PER):
            tile_row = order[step + offset] * PER + i
            left = turned[step * PER + i]
            for slot in range(SLOTS):
                product = jnp.dot(left, tiles[step, i, slot], preferred_element_type=F32)
                place = index[tile_row, slot]
                acc[place] = acc[place] + product
        return carry

    lax.fori_loop(0, count, body, 0)

    if final:
        for b in (1, 2, 3):
            for a in (1, 2, 3):
                turn_block(acc, a, b, many[b - 1], (a - 1) * ND)


def turn_block(acc, a, b, out, start):
    for n in range(PER):
        row = start + n * TILE
        out[row:row + TILE, :] = acc[rel(-a, -b) * PER + n].astype(BF).T


def rest_kernel(acc, own, *sides):
    for a in (1, 2, 3, 0):
        turn_block(acc, a, 0, own, a * ND)
    for b in (1, 2, 3):
        turn_block(acc, 0, b, sides[b - 1], 0)


def backward(offset, order, index, adj, sources, acc=None, final=False):
    width = sources[0].shape[1]
    count = len(sources)
    state = jax.ShapeDtypeStruct((DUMMY + 1, width, TILE), F32)
    outs = (state,)
    if final:
        outs += tuple(jax.ShapeDtypeStruct((n * ND, width), BF) for n in (3, 3, 3))
    initial = acc is None
    extra = [] if initial else [acc]
    return pl.pallas_call(
        functools.partial(backward_kernel, offset, count, initial, final),
        out_shape=outs,
        in_specs=[SM, SM, pl.BlockSpec(memory_space=pltpu.HBM)] + [VM] * (count + len(extra)),
        out_specs=[VM] * len(outs),
        scratch_shapes=[
            pltpu.VMEM((count * PER, width, TILE), BF),
            pltpu.VMEM((count, PER, SLOTS, TILE, TILE), BF),
            pltpu.SemaphoreType.DMA((count,)),
        ],
        input_output_aliases={} if initial else {3 + count: 0},
        compiler_params=params(8),
        cost_estimate=cost(count * PER * SLOTS * 2 * TILE * TILE * width, count * PER * SLOTS * TILE * TILE * 2),
    )(order, index, adj, *sources, *extra)


def add_terms_kernel(*refs):
    terms, out = [ref[...].astype(F32) for ref in refs[:-1]], refs[-1]
    total = sum4(*terms) if len(terms) == SIDE else terms[0] + terms[1]
    wrows = out.shape[0] - BROWS
    out[0:wrows, :] = total[:wrows].astype(BF)
    out[wrows:, :] = pack_bias(jnp.sum(total[wrows:], axis=0, keepdims=True))


def last_terms_kernel(scale, t0, t1, wout, bout):
    total = t0[...].astype(F32) + t1[...].astype(F32)
    wrows = wout.shape[0]
    wout[...] = total[:wrows] * scale
    bout[...] = jnp.sum(total[wrows:], axis=0, keepdims=True) * scale


def small(kernel, outs, operands):
    return pl.pallas_call(
        kernel,
        out_shape=outs,
        in_specs=[VM] * len(operands),
        out_specs=jax.tree.map(lambda _: VM, outs),
        compiler_params=params(8),
    )(*operands)


def relay_kernel(own, r1, r2, r3, *outs):
    for a, out in enumerate(outs):
        total = own[(a + 1) * ND:(a + 2) * ND, :].astype(F32)
        for ref in (r1, r2, r3):
            total = total + ref[a * ND:(a + 1) * ND, :].astype(F32)
        out[...] = total.astype(BF)


def finish_kernel(own, *refs):
    weight, gfeat = refs[-2:]
    total = own[0:ND, :].astype(F32)
    for ref in refs[:-2]:
        total = total + ref[...].astype(F32)
    gfeat[...] = lax.dot_general(
        total.astype(BF), weight[...], (((1,), (1,)), ((), ())), preferred_element_type=F32
    ).astype(BF)


def shards(features, weight, out_bias, cotangent, adj_tiles, tile_cols, tile_counts):
    row = lax.axis_index("row")
    col = lax.axis_index("col")
    x, y, z, k = row // SIDE, row % SIDE, col // 2, col % 2
    width = features.shape[1]
    tile_rows = adj_tiles.shape[2]
    adj = pltpu.with_memory_space_constraint(adj_tiles.reshape(tile_rows, SLOTS, TILE, TILE), pltpu.HBM)
    mark = small(mark_kernel, jax.ShapeDtypeStruct((8, 128), jnp.int32), [])
    place = jnp.stack([x, y, k]).astype(jnp.int32)
    index = pl.pallas_call(
        index_kernel,
        out_shape=jax.ShapeDtypeStruct((tile_rows, SLOTS), jnp.int32),
        in_specs=[SM, VM, VM, VM],
        out_specs=VM,
        compiler_params=params(1),
    )(place, tile_cols.reshape(tile_rows, SLOTS), tile_counts.reshape(tile_rows, 1), mark)
    held = pl.pallas_call(
        load_kernel,
        out_shape=jax.ShapeDtypeStruct(adj.shape, adj.dtype),
        in_specs=[pl.BlockSpec(memory_space=pltpu.HBM)],
        out_specs=VM,
        scratch_shapes=[pltpu.SemaphoreType.DMA((12,))],
        compiler_params=params(1),
    )(adj)
    other = 1 - k
    onward = [(z + d) % SIDE * 2 for d in range(SIDE)]
    back = [(z - d) % SIDE * 2 for d in range(SIDE)]
    order_forward = jnp.stack(
        [v + other for v in onward[1:]] + [v + k for v in onward[1:]] + [onward[0] + other, onward[0] + k]
    ).astype(jnp.int32)
    order_backward = jnp.stack(
        [back[0] + k, back[0] + other] + [v + k for v in back[1:]] + [v + other for v in back[1:]]
    ).astype(jnp.int32)

    def fan(send, values):
        received = []
        for d in (1, 2, 3):
            received.append(send(values[d - 1], d))
        return received

    first = fan(lambda v, d: send_plane(v, True, d), [features] * 3)
    side = fan(lambda v, d: send_plane(v, False, d), [features] * 3)
    line = small(join_kernel, jax.ShapeDtypeStruct((3 * ND, width), BF), first)
    many = fan(lambda v, d: send_plane(v, False, d), [line] * 3)
    swap, panel = forward(0, 3, order_forward, index, held, [features, *first, *side, *many])

    recv = send_col(swap, 0, 1)
    away = forward(3, 3, order_forward, index, held, [panel])
    messages = [(away[d].astype(F32) + recv[d].astype(F32)).astype(BF) for d in range(3)]
    parts = fan(lambda v, d: send_col(v, d, 0), messages)
    keep = forward(6, 2, order_forward, index, held, [panel])
    recv = send_col(keep[0], 0, 1)
    block = jax.ShapeDtypeStruct((ND, width), BF)
    terms = jax.ShapeDtypeStruct((width + BROWS, width), BF)
    activated, grad, along = small(
        activation_kernel,
        (block, block, terms),
        [keep, recv, *parts, weight, out_bias.reshape(1, -1), cotangent],
    )

    mine = [grad] + fan(lambda v, d: send_col(v, d, 0), [grad] * 3)
    theirs = [send_col(grad, 0, 1)]
    theirs += fan(lambda v, d: send_col(v, 0, 1), mine[1:])
    other_terms = trade_row(along, 1, True)
    along = small(add_terms_kernel, terms, [along, other_terms])
    other_terms = trade_row(along, 2, True)
    acc, = backward(0, order_backward, index, adj, [mine[0], theirs[0]])
    along = small(add_terms_kernel, terms, [along, other_terms])
    other_terms = trade_row(along, 1, False)
    acc, = backward(2, order_backward, index, adj, mine[1:], acc)
    along = small(add_terms_kernel, terms, [along, other_terms])
    other_terms = trade_row(along, 2, False)
    acc, *blocks = backward(SIDE + 1, order_backward, index, adj, theirs[1:], acc, final=True)

    landed = fan(lambda v, d: send_plane(v, False, d), blocks)
    own, *blocks = small(rest_kernel, (jax.ShapeDtypeStruct((SIDE * ND, width), BF),) + (block,) * 3, [acc])

    beside = fan(lambda v, d: send_plane(v, False, d), blocks)
    along = small(add_terms_kernel, terms, [along, other_terms])
    along_z = [along] + fan(lambda v, d: send_col(v, d, 0), [along] * 3)
    along = small(add_terms_kernel, terms, along_z)
    other_terms = send_col(along, 0, 1)
    nodes = features.shape[0] * lax.axis_size("row") * lax.axis_size("col")
    grad_weight, grad_bias = small(
        functools.partial(last_terms_kernel, nodes**-0.5),
        (jax.ShapeDtypeStruct((width, width), F32), jax.ShapeDtypeStruct((1, width), F32)),
        [along, other_terms],
    )
    onwards = small(relay_kernel, (block,) * 3, [own, *landed])
    last = fan(lambda v, d: send_plane(v, True, d), onwards)
    grad_features = small(finish_kernel, block, [own, *last, *beside, weight])
    return activated, grad_features, grad_weight, grad_bias.reshape(-1)


def solution(mesh):
    in_specs = (
        P(("row", "col"), None),
        P(),
        P(),
        P(("row", "col"), None),
        P("row", "col", None, None, None, None),
        P("row", "col", None, None),
        P("row", "col", None),
    )
    out_specs = (P(("row", "col"), None), P(("row", "col"), None), P(), P())

    return jax.shard_map(shards, mesh=mesh, in_specs=in_specs, out_specs=out_specs, check_vma=False)
```

```python
import functools

import jax
import jax.numpy as jnp
from jax import lax
from jax.experimental import pallas as pl
from jax.experimental.pallas import tpu as pltpu
from jax.sharding import PartitionSpec as P


TILE = 128
SLOTS = 16
SIDE = 4
ND = 384
PER = ND // TILE
DUMMY = SIDE * SIDE * PER
BROWS = 16
BF = jnp.bfloat16
F32 = jnp.float32
VM = pl.BlockSpec(memory_space=pltpu.VMEM)
SM = pl.BlockSpec(memory_space=pltpu.SMEM)


def send_plane(value, first, step):
    pairs = []
    for row in range(SIDE * SIDE):
        for col in range(2 * SIDE):
            x, y = divmod(row, SIDE)
            if (col % 2 == 0) == first:
                x = (x + step) % SIDE
            else:
                y = (y + step) % SIDE
            pairs.append((row * 2 * SIDE + col, (x * SIDE + y) * 2 * SIDE + col))
    return lax.ppermute(value, ("row", "col"), pairs)


def trade_row(value, bit, along_x):
    pairs = []
    for x in range(SIDE):
        for y in range(SIDE):
            there = ((x ^ bit), y) if along_x else (x, (y ^ bit))
            pairs.append((x * SIDE + y, there[0] * SIDE + there[1]))
    return lax.ppermute(value, "row", pairs)


def send_col(value, dz, dk):
    pairs = []
    for z in range(SIDE):
        for k in range(2):
            pairs.append((z * 2 + k, (z + dz) % SIDE * 2 + (k ^ dk)))
    return lax.ppermute(value, "col", pairs)


def rel(first, second):
    return (second % SIDE) * SIDE + first % SIDE


def params(mb):
    return pltpu.CompilerParams(vmem_limit_bytes=mb * 1024 * 1024)


def cost(flops, data):
    return pl.CostEstimate(flops=flops, bytes_accessed=data, transcendentals=0)


def sum4(a, b, c, d):
    return (a + c) + (b + d)


def pack_bias(total):
    hi = total.astype(BF)
    lo = (total - hi.astype(F32)).astype(BF)
    rows = lax.broadcasted_iota(jnp.int32, (BROWS, total.shape[1]), 0)
    zero = jnp.zeros((BROWS, total.shape[1]), F32)
    return jnp.where(rows == 0, hi.astype(F32), jnp.where(rows == 1, lo.astype(F32), zero)).astype(BF)


def mark_kernel(out):
    out[...] = jnp.zeros_like(out)


def join_kernel(*refs):
    for n, ref in enumerate(refs[:-1]):
        refs[-1][n * ND:(n + 1) * ND, :] = ref[...]


def load_kernel(source, out, sems):
    parts = sems.shape[0]
    chunk = source.shape[0] // parts
    copies = []
    for n in range(parts):
        part = pl.ds(n * chunk, chunk)
        copies.append(pltpu.make_async_copy(source.at[part], out.at[part], sems.at[n]))
    for n in range(parts + 2):
        if n < parts:
            copies[n].start()
        if n >= 2:
            copies[n - 2].wait()


def index_kernel(place, cols, counts, mark, out):
    column = cols[...]
    source = (column * 43) >> 7
    away_x = (place[0] - (source >> 2)) & (SIDE - 1)
    away_y = (place[1] - source) & (SIDE - 1)
    distance = jnp.where(place[2] == 0, away_y * SIDE + away_x, away_x * SIDE + away_y)
    live = lax.broadcasted_iota(jnp.int32, column.shape, 1) < counts[...]
    out[...] = jnp.where(live, distance * PER + (column - source * PER), DUMMY) + mark[0:1, 0:1]


def forward_steps(offset, steps, order, index, adj, panel, out):
    def body(step, carry):
        for i in range(PER):
            tile_row = order[step + offset] * PER + i
            total = None
            for pair in range(SLOTS // 2):
                picked = []
                for half in range(2):
                    start = pl.multiple_of(index[tile_row, 2 * pair + half] * TILE, TILE)
                    picked.append(panel[pl.ds(start, TILE), :])
                left = jnp.concatenate([adj[tile_row, 2 * pair], adj[tile_row, 2 * pair + 1]], axis=1)
                product = jnp.dot(left, jnp.concatenate(picked, axis=0), preferred_element_type=F32)
                total = product if total is None else total + product
            out[step, i * TILE:(i + 1) * TILE, :] = total.astype(BF)
        return carry

    lax.fori_loop(0, steps, body, 0)


def forward_first_kernel(offset, steps, order, index, adj, own, f1, f2, f3, s1, s2, s3, m1, m2, m3, out, panel):
    panel[0:ND, :] = own[...]
    for a, ref in enumerate((f1, f2, f3)):
        panel[rel(a + 1, 0) * ND:(rel(a + 1, 0) + 1) * ND, :] = ref[...]
    for b, (side, many) in enumerate(((s1, m1), (s2, m2), (s3, m3))):
        start = rel(0, b + 1) * ND
        panel[start:start + ND, :] = side[...]
        panel[start + ND:start + SIDE * ND, :] = many[...]
    panel[DUMMY * TILE:, :] = jnp.zeros((TILE, panel.shape[1]), BF)
    forward_steps(offset, steps, order, index, adj, panel, out)


def forward(offset, steps, order, index, adj, operands):
    width = operands[0].shape[1]
    first = len(operands) > 1
    shape = jax.ShapeDtypeStruct((steps, ND, width), BF)
    panel = jax.ShapeDtypeStruct(((DUMMY + 1) * TILE, width), BF)
    return pl.pallas_call(
        functools.partial(forward_first_kernel if first else forward_steps, offset, steps),
        out_shape=(shape, panel) if first else shape,
        in_specs=[SM, SM] + [VM] * (1 + len(operands)),
        out_specs=(VM, VM) if first else VM,
        compiler_params=params(6),
        cost_estimate=cost(steps * PER * SLOTS * 2 * TILE * TILE * width, steps * PER * SLOTS * TILE * TILE * 2),
    )(order, index, adj, *operands)


def activation_kernel(keep, recv, r1, r2, r3, weight, bias, cot, act, grad_out, both):
    agg = keep[1].astype(F32) + recv[...].astype(F32)
    for ref in (r1, r2, r3):
        agg = agg + ref[...].astype(F32)
    agg16 = agg.astype(BF)
    pre = jnp.dot(agg16, weight[...], preferred_element_type=F32) + bias[...]
    sig = 1.0 / (1.0 + jnp.exp(-pre))
    act[...] = (pre * sig).astype(BF)
    grad = (cot[...].astype(F32) * sig * (1.0 + pre * (1.0 - sig))).astype(BF)
    grad_out[...] = grad
    both[0:ND, :] = grad
    wrows = both.shape[0] - BROWS
    both[ND:wrows, :] = lax.dot_general(
        agg16, grad, (((0,), (0,)), ((), ())), preferred_element_type=F32
    ).astype(BF)
    both[wrows:, :] = pack_bias(jnp.sum(grad.astype(F32), axis=0, keepdims=True))


def backward_kernel(offset, count, initial, final, order, index, adj, *refs):
    sources, refs = refs[:count], refs[count:]
    if not initial:
        refs = refs[1:]
    acc, refs = refs[0], refs[1:]
    if final:
        many = refs[:3]
    turned, tiles, sems = refs[-3:]

    def fetch(step):
        rows = pl.ds(order[step + offset] * PER, PER)
        return pltpu.make_async_copy(adj.at[rows], tiles.at[step], sems.at[step])

    for step in range(count):
        fetch(step).start()
    for s, ref in enumerate(sources):
        for i in range(PER):
            turned[s * PER + i] = ref[i * TILE:(i + 1) * TILE, :].T
    if initial:
        acc[...] = jnp.zeros_like(acc)

    def body(step, carry):
        fetch(step).wait()
        for i in range(PER):
            tile_row = order[step + offset] * PER + i
            left = turned[step * PER + i]
            for slot in range(SLOTS):
                product = jnp.dot(left, tiles[step, i, slot], preferred_element_type=F32)
                place = index[tile_row, slot]
                acc[place] = acc[place] + product
        return carry

    lax.fori_loop(0, count, body, 0)

    if final:
        for b in (1, 2, 3):
            for a in (1, 2, 3):
                turn_block(acc, a, b, many[b - 1], (a - 1) * ND)


def turn_block(acc, a, b, out, start):
    for n in range(PER):
        row = start + n * TILE
        out[row:row + TILE, :] = acc[rel(-a, -b) * PER + n].astype(BF).T


def rest_kernel(acc, own, *sides):
    for a in (1, 2, 3, 0):
        turn_block(acc, a, 0, own, a * ND)
    for b in (1, 2, 3):
        turn_block(acc, 0, b, sides[b - 1], 0)


def backward(offset, order, index, adj, sources, acc=None, final=False):
    width = sources[0].shape[1]
    count = len(sources)
    state = jax.ShapeDtypeStruct((DUMMY + 1, width, TILE), F32)
    outs = (state,)
    if final:
        outs += tuple(jax.ShapeDtypeStruct((n * ND, width), BF) for n in (3, 3, 3))
    initial = acc is None
    extra = [] if initial else [acc]
    return pl.pallas_call(
        functools.partial(backward_kernel, offset, count, initial, final),
        out_shape=outs,
        in_specs=[SM, SM, pl.BlockSpec(memory_space=pltpu.HBM)] + [VM] * (count + len(extra)),
        out_specs=[VM] * len(outs),
        scratch_shapes=[
            pltpu.VMEM((count * PER, width, TILE), BF),
            pltpu.VMEM((count, PER, SLOTS, TILE, TILE), BF),
            pltpu.SemaphoreType.DMA((count,)),
        ],
        input_output_aliases={} if initial else {3 + count: 0},
        compiler_params=params(8),
        cost_estimate=cost(count * PER * SLOTS * 2 * TILE * TILE * width, count * PER * SLOTS * TILE * TILE * 2),
    )(order, index, adj, *sources, *extra)


def add_terms_kernel(*refs):
    terms, out = [ref[...].astype(F32) for ref in refs[:-1]], refs[-1]
    total = sum4(*terms) if len(terms) == SIDE else terms[0] + terms[1]
    wrows = out.shape[0] - BROWS
    out[0:wrows, :] = total[:wrows].astype(BF)
    out[wrows:, :] = pack_bias(jnp.sum(total[wrows:], axis=0, keepdims=True))


def pair_terms_kernel(mine, theirs, out):
    total = mine[ND:, :].astype(F32) + theirs[ND:, :].astype(F32)
    wrows = out.shape[0] - BROWS
    out[0:wrows, :] = total[:wrows].astype(BF)
    out[wrows:, :] = pack_bias(jnp.sum(total[wrows:], axis=0, keepdims=True))


def last_terms_kernel(scale, t0, t1, wout, bout):
    total = t0[...].astype(F32) + t1[...].astype(F32)
    wrows = wout.shape[0]
    wout[...] = total[:wrows] * scale
    bout[...] = jnp.sum(total[wrows:], axis=0, keepdims=True) * scale


def small(kernel, outs, operands):
    return pl.pallas_call(
        kernel,
        out_shape=outs,
        in_specs=[VM] * len(operands),
        out_specs=jax.tree.map(lambda _: VM, outs),
        compiler_params=params(8),
    )(*operands)


def relay_kernel(own, r1, r2, r3, *outs):
    for a, out in enumerate(outs):
        total = own[(a + 1) * ND:(a + 2) * ND, :].astype(F32)
        for ref in (r1, r2, r3):
            total = total + ref[a * ND:(a + 1) * ND, :].astype(F32)
        out[...] = total.astype(BF)


def finish_kernel(own, *refs):
    weight, gfeat = refs[-2:]
    total = own[0:ND, :].astype(F32)
    for ref in refs[:-2]:
        total = total + ref[...].astype(F32)
    gfeat[...] = lax.dot_general(
        total.astype(BF), weight[...], (((1,), (1,)), ((), ())), preferred_element_type=F32
    ).astype(BF)


def shards(features, weight, out_bias, cotangent, adj_tiles, tile_cols, tile_counts):
    row = lax.axis_index("row")
    col = lax.axis_index("col")
    x, y, z, k = row // SIDE, row % SIDE, col // 2, col % 2
    width = features.shape[1]
    tile_rows = adj_tiles.shape[2]
    adj = pltpu.with_memory_space_constraint(adj_tiles.reshape(tile_rows, SLOTS, TILE, TILE), pltpu.HBM)
    mark = small(mark_kernel, jax.ShapeDtypeStruct((8, 128), jnp.int32), [])
    place = jnp.stack([x, y, k]).astype(jnp.int32)
    index = pl.pallas_call(
        index_kernel,
        out_shape=jax.ShapeDtypeStruct((tile_rows, SLOTS), jnp.int32),
        in_specs=[SM, VM, VM, VM],
        out_specs=VM,
        compiler_params=params(1),
    )(place, tile_cols.reshape(tile_rows, SLOTS), tile_counts.reshape(tile_rows, 1), mark)
    held = pl.pallas_call(
        load_kernel,
        out_shape=jax.ShapeDtypeStruct(adj.shape, adj.dtype),
        in_specs=[pl.BlockSpec(memory_space=pltpu.HBM)],
        out_specs=VM,
        scratch_shapes=[pltpu.SemaphoreType.DMA((12,))],
        compiler_params=params(1),
    )(adj)
    other = 1 - k
    onward = [(z + d) % SIDE * 2 for d in range(SIDE)]
    back = [(z - d) % SIDE * 2 for d in range(SIDE)]
    order_forward = jnp.stack(
        [v + other for v in onward[1:]] + [v + k for v in onward[1:]] + [onward[0] + other, onward[0] + k]
    ).astype(jnp.int32)
    order_backward = jnp.stack(
        [back[0] + k, back[0] + other] + [v + k for v in back[1:]] + [v + other for v in back[1:]]
    ).astype(jnp.int32)

    def fan(send, values):
        received = []
        for d in (1, 2, 3):
            received.append(send(values[d - 1], d))
        return received

    first = fan(lambda v, d: send_plane(v, True, d), [features] * 3)
    side = fan(lambda v, d: send_plane(v, False, d), [features] * 3)
    line = small(join_kernel, jax.ShapeDtypeStruct((3 * ND, width), BF), first)
    many = fan(lambda v, d: send_plane(v, False, d), [line] * 3)
    swap, panel = forward(0, 3, order_forward, index, held, [features, *first, *side, *many])

    recv = send_col(swap, 0, 1)
    away = forward(3, 3, order_forward, index, held, [panel])
    messages = [(away[d].astype(F32) + recv[d].astype(F32)).astype(BF) for d in range(3)]
    parts = fan(lambda v, d: send_col(v, d, 0), messages)
    keep = forward(6, 2, order_forward, index, held, [panel])
    recv = send_col(keep[0], 0, 1)
    block = jax.ShapeDtypeStruct((ND, width), BF)
    terms = jax.ShapeDtypeStruct((width + BROWS, width), BF)
    both = jax.ShapeDtypeStruct((ND + width + BROWS, width), BF)
    activated, grad, both = small(
        activation_kernel,
        (block, block, both),
        [keep, recv, *parts, weight, out_bias.reshape(1, -1), cotangent],
    )

    mine = [grad] + fan(lambda v, d: send_col(v, d, 0), [grad] * 3)
    theirs = [send_col(both, 0, 1)]
    along = small(pair_terms_kernel, terms, [both, theirs[0]])
    theirs += fan(lambda v, d: send_col(v, 0, 1), mine[1:])
    other_terms = trade_row(along, 1, True)
    acc, = backward(0, order_backward, index, adj, [mine[0], theirs[0]])
    along = small(add_terms_kernel, terms, [along, other_terms])
    other_terms = trade_row(along, 2, True)
    acc, = backward(2, order_backward, index, adj, mine[1:], acc)
    along = small(add_terms_kernel, terms, [along, other_terms])
    other_terms = trade_row(along, 1, False)
    acc, *blocks = backward(SIDE + 1, order_backward, index, adj, theirs[1:], acc, final=True)

    landed = fan(lambda v, d: send_plane(v, False, d), blocks)
    own, *blocks = small(rest_kernel, (jax.ShapeDtypeStruct((SIDE * ND, width), BF),) + (block,) * 3, [acc])

    beside = fan(lambda v, d: send_plane(v, False, d), blocks)
    along = small(add_terms_kernel, terms, [along, other_terms])
    along_z = [along] + fan(lambda v, d: send_col(v, d, 0), [along] * 3)
    along = small(add_terms_kernel, terms, along_z)
    other_terms = trade_row(along, 2, False)
    nodes = features.shape[0] * lax.axis_size("row") * lax.axis_size("col")
    grad_weight, grad_bias = small(
        functools.partial(last_terms_kernel, nodes**-0.5),
        (jax.ShapeDtypeStruct((width, width), F32), jax.ShapeDtypeStruct((1, width), F32)),
        [along, other_terms],
    )
    onwards = small(relay_kernel, (block,) * 3, [own, *landed])
    last = fan(lambda v, d: send_plane(v, True, d), onwards)
    grad_features = small(finish_kernel, block, [own, *last, *beside, weight])
    return activated, grad_features, grad_weight, grad_bias.reshape(-1)


def solution(mesh):
    in_specs = (
        P(("row", "col"), None),
        P(),
        P(),
        P(("row", "col"), None),
        P("row", "col", None, None, None, None),
        P("row", "col", None, None),
        P("row", "col", None),
    )
    out_specs = (P(("row", "col"), None), P(("row", "col"), None), P(), P())

    return jax.shard_map(shards, mesh=mesh, in_specs=in_specs, out_specs=out_specs, check_vma=False)
```
